32 devices in a mesh: section: 4 (over z), dp: 4 (over y, x), hid: 2 (over core).
Axes of the slice: x: 2, y: 2, z: 4, core: 2. Of those that a mesh axis runs over, the one named last changes fastest.
Arguments:
- forward_input: bfloat16 [4, 768, 2048], P('section', 'dp'), may hold values from -6 to 6
- backward_input: bfloat16 [4, 768, 2048], P('section', 'dp'), may hold values from -6 to 6
- output_grad: bfloat16 [4, 768, 2048], P('section', 'dp'), may hold values from -8 to 8
- norm_gain: float32 [4, 2048], P('section'), may hold values from 0.5 to 1.5
- in_weight: float32 [4, 2, 2048, 512], P('section', None, 'dp', 'hid'), may hold values from -0.125 to 0.125
- out_weight: float32 [4, 512, 2048], P('section', 'hid', 'dp'), may hold values from -0.25 to 0.25
- in_codes: int32 [4, 2, 2048, 512], P('section', None, 'dp', 'hid'), may hold values from 0 to 32511
- out_codes: int32 [4, 512, 2048], P('section', 'hid', 'dp'), may hold values from 0 to 32511
- in_scales: float32 [4, 2, 2, 2048, 2], P('section', None, None, 'dp', 'hid'), may hold values from 0.005 to 0.05
- out_scales: float32 [4, 2, 2, 2048], P('section', None, 'hid', 'dp'), may hold values from 0.005 to 0.05
- section_lags: int32 [4], P('section'), may hold values from 1 to 4
Outputs:
- next_input: bfloat16 [4, 768, 2048], P('section', 'dp')
- input_grad: bfloat16 [4, 768, 2048], P('section', 'dp')
- in_update: float32 [4, 2, 2048, 512], P('section', None, 'dp', 'hid')
- out_update: float32 [4, 512, 2048], P('section', 'hid', 'dp')
The draws below stay inside these ranges and needn't reach their ends.
Inputs may be any that keep to these rules, and one draw needn't show every extreme that they name: `in_codes`: each code holds a first-moment code of 0 to 126 times 256 plus a second-moment code of 0 to 255. `out_codes`: each code holds a first-moment code of 0 to 126 times 256 plus a second-moment code of 0 to 255.
All inputs are finite; a program needn't handle non-finite values.
Results may differ from the reference program's by a relative error of at most 0.012.
Values may be sent and summed in bfloat16 or wider, within the bound.
A program may use at most 64 MiB of HBM per device.

```python
import math
import jax
import jax.numpy as jnp
from jax import lax

D = 2048
FF = 512
ROWS = 192
QB = 256
STEP = 1000
SECTIONS = 4
ROWS_ALL = 768
N_HID = 2


def set_ends(values, stream_key, low, top_value):
    extent = values.shape
    spot = [jax.random.randint(jax.random.fold_in(stream_key, axis), (), 0, extent[axis]) for axis in range(len(extent))]
    values = values.at[tuple(spot)].set(low)
    longest = extent.index(max(extent))
    spot[longest] = (spot[longest] + 1) % extent[longest]
    return values.at[tuple(spot)].set(top_value)


def raised(entries, rng, source, target, blocks, factor):
    def block_of(dim):
        return (jnp.arange(entries.shape[dim]) // (entries.shape[dim] // blocks)).reshape((-1,) + (1,) * (entries.ndim - 1 - dim))

    one_side = jax.random.permutation(rng, blocks)[block_of(target)]
    far = (block_of(target) + blocks // 2) % blocks
    return jnp.where((block_of(source) == one_side) | (block_of(source) == far), factor * entries, entries)


def shard_levels(own_key, dims, pieces, least, largest):
    factor_of = 1.0
    for position, blocks in pieces:
        steps = jax.random.uniform(jax.random.fold_in(jax.random.fold_in(own_key, 6), position), (blocks,), jnp.float32, least / len(pieces), largest / len(pieces))
        factor_of = factor_of * jnp.repeat(jnp.exp(steps), dims[position] // blocks).reshape((-1,) + (1,) * (len(dims) - 1 - position))
    return factor_of


def scatter_about(stream_key, shape, deviation, reach, shards=(), held_as=jnp.bfloat16):
    array = jax.random.normal(stream_key, shape, jnp.float32) * deviation
    if len(shards) > 0:
        array = shard_levels(stream_key, shape, shards, -0.22, 0.18) * array
    return jnp.clip(array, min=-reach, max=reach).astype(held_as)


def noise_with(key, dims, width, most, shards, heavy, dtype=jnp.bfloat16):
    array = width * jax.random.normal(key, dims, jnp.float32)
    if shards:
        array = array * shard_levels(key, dims, shards, -0.22, 0.18)
    return jnp.clip(raised(array, jax.random.fold_in(key, 3), *heavy), -most, most).astype(dtype)


def setup_inputs(seed: int = 0) -> dict:
    key_of = jax.random.split(jax.random.key(seed), 12)
    return {
        "forward_input": scatter_about(key_of[0], (SECTIONS, ROWS_ALL, D), 1.0, 6.0, ((0, 4), (1, 4))),
        "backward_input": scatter_about(key_of[1], (SECTIONS, ROWS_ALL, D), 1.0, 6.0, ((0, 4), (1, 4))),
        "output_grad": noise_with(key_of[2], (SECTIONS, ROWS_ALL, D), 1.0, 8.0, ((0, 4), (1, 4)), (1, 2, 4, 2.0)),
        "norm_gain": jnp.clip(1.0 + 0.1 * jax.random.normal(key_of[3], (SECTIONS, D), jnp.float32), 0.5, 1.5),
        "in_weight": scatter_about(key_of[4], (SECTIONS, 2, D, FF), D ** -0.5, 0.125, ((0, 4), (2, 4), (3, 2)), jnp.float32),
        "out_weight": scatter_about(key_of[5], (SECTIONS, FF, D), FF ** -0.5, 0.25, ((0, 4), (1, 2), (2, 4)), jnp.float32),
        "in_codes": set_ends(jax.random.randint(key_of[6], (SECTIONS, 2, D, FF), 0, 32512), jax.random.fold_in(key_of[6], 1), 0, 32511).astype(jnp.int32),
        "out_codes": set_ends(jax.random.randint(key_of[7], (SECTIONS, FF, D), 0, 32512), jax.random.fold_in(key_of[7], 1), 0, 32511).astype(jnp.int32),
        "in_scales": jnp.clip(jnp.exp(math.log(0.05) - 2.3025851 * jax.random.uniform(key_of[8], (SECTIONS, 2, 2, D, FF // QB), jnp.float32) ** shard_levels(key_of[8], (SECTIONS, 2, 2, D, FF // QB), ((0, 4), (3, 4), (4, 2)), -0.2, 0.2)), 0.005, 0.05),
        "out_scales": jnp.clip(jnp.exp(math.log(0.05) - 2.3025851 * jax.random.uniform(key_of[9], (SECTIONS, 2, FF // QB, D), jnp.float32) ** shard_levels(key_of[9], (SECTIONS, 2, FF // QB, D), ((0, 4), (2, 2), (3, 4)), -0.2, 0.2)), 0.005, 0.05),
        "section_lags": set_ends(jax.random.randint(key_of[10], (SECTIONS,), 1, 5), jax.random.fold_in(key_of[10], 1), 1, 4).astype(jnp.int32),
    }


BETA_ONE = 0.9
BETA_TWO = 0.999
ADAM_EPS = 1e-08
NORM_EPS = 1e-06
LEARN_RATE = 0.003

def dequant(codes, first_scale, second_scale):
    high = (codes // 256).astype(jnp.float32)
    low = (codes % 256).astype(jnp.float32)
    moment_m = first_scale * (high - 63.0) / 63.0
    moment_v = jnp.square(second_scale * (0.25 + 0.75 * low / 255.0))
    return (moment_m, moment_v)

def direction(moment_m, moment_v, count):
    return moment_m / (1.0 - BETA_ONE ** count) / (jnp.sqrt(moment_v / (1.0 - BETA_TWO ** count)) + ADAM_EPS)

def normalize(inputs, gain):
    values = inputs.astype(jnp.float32)
    factor = lax.rsqrt(lax.optimization_barrier(jnp.mean(values * values, axis=-1, keepdims=True)) + NORM_EPS)
    return ((values * factor * gain).astype(jnp.bfloat16), factor, values)

def one_section(items):
    fwd_rows, bwd_rows, out_cot, gain, w_in, w_out, c_in, c_out, s_in, s_out, lag_count = items
    lag_value = lag_count.astype(jnp.float32)
    m_in, v_in = dequant(c_in, jnp.repeat(s_in[0], QB, axis=-1), jnp.repeat(s_in[1], QB, axis=-1))
    m_out, v_out = dequant(c_out, jnp.repeat(s_out[0], QB, axis=0), jnp.repeat(s_out[1], QB, axis=0))
    pred_in = (w_in - LEARN_RATE * lag_value * direction(m_in, v_in, STEP - 1)).astype(jnp.bfloat16)
    pred_out = (w_out - LEARN_RATE * lag_value * direction(m_out, v_out, STEP - 1)).astype(jnp.bfloat16)
    rows_all = fwd_rows.shape[0]
    half_ff = FF // N_HID
    hp = lax.Precision.HIGHEST
    normed, factor, values = normalize(fwd_rows, gain)
    gate_val = jnp.dot(normed, pred_in[0], preferred_element_type=jnp.float32)
    up_val = jnp.dot(normed, pred_in[1], preferred_element_type=jnp.float32)
    hidden = (gate_val * jax.nn.sigmoid(gate_val) * up_val).astype(jnp.bfloat16)
    parts = jnp.einsum('rkf,kfd->krd', hidden.reshape(rows_all, N_HID, half_ff).astype(jnp.float32), pred_out.reshape(N_HID, half_ff, D).astype(jnp.float32), precision=hp)
    summed = lax.optimization_barrier(jnp.sum(parts.astype(jnp.bfloat16).astype(jnp.float32), axis=0))
    ahead = (values + summed).astype(jnp.bfloat16)
    normed_b, factor_b, values_b = normalize(bwd_rows, gain)
    gate_b = jnp.dot(normed_b, pred_in[0], preferred_element_type=jnp.float32)
    up_b = jnp.dot(normed_b, pred_in[1], preferred_element_type=jnp.float32)
    sig_b = jax.nn.sigmoid(gate_b)
    hidden_b = (gate_b * sig_b * up_b).astype(jnp.bfloat16)
    grad_h = jnp.dot(out_cot, pred_out.T, preferred_element_type=jnp.float32)
    grad_gate = (grad_h * up_b * sig_b * (1.0 + gate_b * (1.0 - sig_b))).astype(jnp.bfloat16)
    grad_up = (grad_h * gate_b * sig_b).astype(jnp.bfloat16)
    gate_parts = jnp.einsum('rkf,dkf->krd', grad_gate.reshape(rows_all, N_HID, half_ff).astype(jnp.float32), pred_in[0].reshape(D, N_HID, half_ff).astype(jnp.float32), precision=hp)
    up_parts = jnp.einsum('rkf,dkf->krd', grad_up.reshape(rows_all, N_HID, half_ff).astype(jnp.float32), pred_in[1].reshape(D, N_HID, half_ff).astype(jnp.float32), precision=hp)
    grad_n = lax.optimization_barrier(jnp.sum((gate_parts + up_parts).astype(jnp.bfloat16).astype(jnp.float32), axis=0))
    scaled = gain * grad_n
    grad_x = out_cot.astype(jnp.float32) + factor_b * scaled - values_b * factor_b ** 3 * lax.optimization_barrier(jnp.mean(scaled * values_b, axis=-1, keepdims=True))
    back_rows = grad_x.astype(jnp.bfloat16)
    groups = rows_all // ROWS
    n_grp = normed_b.reshape(groups, ROWS, D).astype(jnp.float32)
    g_grp = grad_gate.reshape(groups, ROWS, FF).astype(jnp.float32)
    u_grp = grad_up.reshape(groups, ROWS, FF).astype(jnp.float32)
    h_grp = hidden_b.reshape(groups, ROWS, FF).astype(jnp.float32)
    y_grp = out_cot.reshape(groups, ROWS, D).astype(jnp.float32)

    def group_sum(left, right, form):
        terms = jnp.einsum(form, left, right, precision=hp)
        return lax.optimization_barrier(jnp.sum(terms.astype(jnp.bfloat16).astype(jnp.float32), axis=0)) / rows_all
    grad_in = jnp.stack([group_sum(n_grp, g_grp, 'srd,srf->sdf'), group_sum(n_grp, u_grp, 'srd,srf->sdf')])
    grad_out = group_sum(h_grp, y_grp, 'srf,srd->sfd')
    new_m_in = BETA_ONE * m_in + (1.0 - BETA_ONE) * grad_in
    new_v_in = BETA_TWO * v_in + (1.0 - BETA_TWO) * grad_in * grad_in
    new_m_out = BETA_ONE * m_out + (1.0 - BETA_ONE) * grad_out
    new_v_out = BETA_TWO * v_out + (1.0 - BETA_TWO) * grad_out * grad_out
    return (ahead, back_rows, direction(new_m_in, new_v_in, STEP), direction(new_m_out, new_v_out, STEP))

def reference(forward_input, backward_input, output_grad, norm_gain, in_weight, out_weight, in_codes, out_codes, in_scales, out_scales, section_lags):
    ahead, back_rows, in_update, out_update = lax.map(one_section, (forward_input, backward_input, output_grad, norm_gain, in_weight, out_weight, in_codes, out_codes, in_scales, out_scales, section_lags))
    zero_rows = jnp.zeros_like(ahead[:1])
    next_input = jnp.concatenate([zero_rows, ahead[:-1]], axis=0)
    input_grad = jnp.concatenate([back_rows[1:], zero_rows], axis=0)
    return (next_input, input_grad, in_update, out_update)
```

```python
import functools
import math

import jax
import jax.numpy as jnp
from jax import lax
from jax.experimental import pallas as pl
from jax.experimental.pallas import tpu as pltpu
from jax.sharding import PartitionSpec as P

QB = 256
STEP = 1000


BETA_ONE = 0.9
BETA_TWO = 0.999
ADAM_EPS = 1e-08
NORM_EPS = 1e-06
LEARN_RATE = 0.003
MESH = pl.DeviceIdType.MESH
CHUNKS = 2


def passed_along(block, axis, distance):
    devices = range(lax.axis_size(axis))
    route = [(i - distance, i) for i in devices if i - distance in devices]
    return lax.ppermute(block, axis, route)


def dequant(codes, first_scale, second_scale):
    high = (codes // 256).astype(jnp.float32)
    low = (codes % 256).astype(jnp.float32)
    moment_m = first_scale * (high - 63.0) / 63.0
    moment_v = jnp.square(second_scale * (0.25 + 0.75 * low / 255.0))
    return (moment_m, moment_v)


def direction(moment_m, moment_v, count):
    return (
        moment_m
        / (1.0 - BETA_ONE**count)
        / (jnp.sqrt(moment_v / (1.0 - BETA_TWO**count)) + ADAM_EPS)
    )


def normalize(inputs, gain):
    values = inputs.astype(jnp.float32)
    factor = lax.rsqrt(jnp.mean(values * values, axis=-1, keepdims=True) + NORM_EPS)
    return ((values * factor * gain).astype(jnp.bfloat16), factor, values)


def local(
    forward_input,
    backward_input,
    output_grad,
    norm_gain,
    in_weight,
    out_weight,
    in_codes,
    out_codes,
    in_scales,
    out_scales,
    section_lags,
):
    lag_value = section_lags[0].astype(jnp.float32)
    gain = norm_gain[0]
    m_in, v_in = dequant(
        in_codes[0],
        jnp.repeat(in_scales[0, 0], QB, axis=-1),
        jnp.repeat(in_scales[0, 1], QB, axis=-1),
    )
    m_out, v_out = dequant(
        out_codes[0],
        jnp.repeat(out_scales[0, 0], QB, axis=0),
        jnp.repeat(out_scales[0, 1], QB, axis=0),
    )
    pred_in = (in_weight[0] - LEARN_RATE * lag_value * direction(m_in, v_in, STEP - 1)).astype(
        jnp.bfloat16
    )
    pred_out = (out_weight[0] - LEARN_RATE * lag_value * direction(m_out, v_out, STEP - 1)).astype(
        jnp.bfloat16
    )
    full_in, full_out = (
        lax.all_gather(pred_in, "dp", axis=1, tiled=True),
        lax.all_gather(pred_out, "dp", axis=1, tiled=True),
    )
    normed, factor, values = normalize(forward_input[0], gain)
    gate_val = jnp.dot(normed, full_in[0], preferred_element_type=jnp.float32)
    up_val = jnp.dot(normed, full_in[1], preferred_element_type=jnp.float32)
    hidden = (gate_val * jax.nn.sigmoid(gate_val) * up_val).astype(jnp.bfloat16)
    partial_value = jnp.dot(hidden, full_out, preferred_element_type=jnp.float32)
    back_in, back_out = (full_in, full_out)
    out_cot = output_grad[0]
    normed_b, factor_b, values_b = normalize(backward_input[0], gain)
    gate_b = jnp.dot(normed_b, back_in[0], preferred_element_type=jnp.float32)
    up_b = jnp.dot(normed_b, back_in[1], preferred_element_type=jnp.float32)
    sig_b = jax.nn.sigmoid(gate_b)
    hidden_b = (gate_b * sig_b * up_b).astype(jnp.bfloat16)
    grad_h = jnp.dot(out_cot, back_out.T, preferred_element_type=jnp.float32)
    grad_gate = (grad_h * up_b * sig_b * (1.0 + gate_b * (1.0 - sig_b))).astype(jnp.bfloat16)
    grad_up = (grad_h * gate_b * sig_b).astype(jnp.bfloat16)
    grad_part = jnp.dot(grad_gate, back_in[0].T, preferred_element_type=jnp.float32) + jnp.dot(
        grad_up, back_in[1].T, preferred_element_type=jnp.float32
    )
    summed, grad_n = (
        lax.psum(partial_value.astype(jnp.bfloat16), "hid").astype(jnp.float32),
        lax.psum(grad_part.astype(jnp.bfloat16), "hid").astype(jnp.float32),
    )
    ahead = (values + summed).astype(jnp.bfloat16)
    next_rows = passed_along(ahead, "section", 1)
    scaled = gain * grad_n
    grad_x = (
        out_cot.astype(jnp.float32)
        + factor_b * scaled
        - values_b * factor_b**3 * jnp.mean(scaled * values_b, axis=-1, keepdims=True)
    )
    back_rows = passed_along(grad_x.astype(jnp.bfloat16), "section", -1)
    local_in = jnp.stack(
        [
            jnp.dot(normed_b.T, grad_gate, preferred_element_type=jnp.float32),
            jnp.dot(normed_b.T, grad_up, preferred_element_type=jnp.float32),
        ]
    )
    local_out = jnp.dot(hidden_b.T, out_cot, preferred_element_type=jnp.float32)
    sum_in, sum_out = (
        lax.psum_scatter(
            local_in.astype(jnp.bfloat16), "dp", scatter_dimension=1, tiled=True
        ).astype(jnp.float32),
        lax.psum_scatter(
            local_out.astype(jnp.bfloat16), "dp", scatter_dimension=1, tiled=True
        ).astype(jnp.float32),
    )
    rows_all = out_cot.shape[0] * lax.axis_size("dp")
    grad_in = sum_in / rows_all
    grad_out = sum_out / rows_all
    new_m_in = BETA_ONE * m_in + (1.0 - BETA_ONE) * grad_in
    new_v_in = BETA_TWO * v_in + (1.0 - BETA_TWO) * grad_in * grad_in
    new_m_out = BETA_ONE * m_out + (1.0 - BETA_ONE) * grad_out
    new_v_out = BETA_TWO * v_out + (1.0 - BETA_TWO) * grad_out * grad_out
    in_update = direction(new_m_in, new_v_in, STEP)
    out_update = direction(new_m_out, new_v_out, STEP)
    return (next_rows[None], back_rows[None], in_update[None], out_update[None])


def matmul(a, b):
    return jnp.dot(a, b, preferred_element_type=jnp.float32)


def matmul_nt(a, b):
    return lax.dot_general(a, b, (((1,), (1,)), ((), ())), preferred_element_type=jnp.float32)


def matmul_tn(a, b):
    return lax.dot_general(a, b, (((0,), (0,)), ((), ())), preferred_element_type=jnp.float32)


def moments(codes, first_scale, second_scale):
    high = (codes >> 8).astype(jnp.float32)
    low = (codes & 255).astype(jnp.float32)
    moment_m = first_scale * ((high - 63.0) * (1.0 / 63.0))
    root_v = second_scale * (0.25 + low * (0.75 / 255.0))
    return moment_m, root_v


def predicted(weight, codes, first_scale, second_scale, step):
    moment_m, root_v = moments(codes, first_scale, second_scale)
    count = STEP - 1
    top = moment_m * (step / (1.0 - BETA_ONE**count))
    bottom = root_v * (1.0 / math.sqrt(1.0 - BETA_TWO**count)) + ADAM_EPS
    return (weight - top / bottom).astype(jnp.bfloat16)


def updated(grad, codes, first_scale, second_scale):
    moment_m, root_v = moments(codes, first_scale, second_scale)
    new_m = BETA_ONE * moment_m + (1.0 - BETA_ONE) * grad
    new_v = BETA_TWO * (root_v * root_v) + (1.0 - BETA_TWO) * grad * grad
    bottom = jnp.sqrt(new_v * (1.0 / (1.0 - BETA_TWO**STEP))) + ADAM_EPS
    return new_m * (1.0 / (1.0 - BETA_ONE**STEP)) / bottom


def tick_kernel(
    n_sec,
    lag_ref, gain_ref, s_in_ref, s_out_ref,
    xf_hbm, xb_hbm, dy_hbm, w_in_hbm, w_out_hbm, c_in_hbm, c_out_hbm,
    y_out, dx_out, u_in_out, u_out_out,
    xf, xb, dy, w_in, w_out, c_in, c_out, s_t,
    p_in, p_out, nrm, acc, dh, hid, dgdu, h_all, n_all, dy_all,
    q_s, q_r, e_s, e_r, y_s, dx_s, y_b, dx_b, g_in, g_out,
    load_sem, store_sem, send_sem, recv_sem,
):
    sec = lax.axis_index("section")
    me = lax.axis_index("dp")
    core = lax.axis_index("hid")
    n_dp, rows, cols = xf.shape
    ff = w_out.shape[0]
    half_r = rows // 2
    me_x = me + 1 - 2 * (me % 2)
    me_y = (me + 2) % 4
    me_d = 3 - me
    owners = (me, me_x, me_y, me_d)
    dev_x, dev_y, dev_d = ((sec, o, core) for o in owners[1:])
    sibling = (sec, me, 1 - core)
    above = (sec + 1, me, core)
    below = (sec - 1, me, core)

    ids = iter(range(send_sem.shape[0]))

    def remote(src, dst, dev):
        i = next(ids)
        return pltpu.make_async_remote_copy(
            src_ref=src, dst_ref=dst, send_sem=send_sem.at[i], recv_sem=recv_sem.at[i],
            device_id=dev, device_id_type=MESH,
        )

    lids = iter(range(load_sem.shape[0]))

    def load(src, dst):
        copy = pltpu.make_async_copy(src, dst, load_sem.at[next(lids)])
        copy.start()
        return copy

    def load_cols(src, dst):
        return [load(src.at[:, pl.ds(j * cols, cols)], dst.at[j]) for j in range(n_dp)]

    l_in = [load(c_in_hbm, c_in), load(w_in_hbm, w_in)]
    l_out = [load(c_out_hbm, c_out), load(w_out_hbm, w_out)]
    l_xb = load_cols(xb_hbm, xb)
    l_xf = load_cols(xf_hbm, xf)
    l_dy = load_cols(dy_hbm, dy)

    barrier = pltpu.get_barrier_semaphore()
    for dev in (dev_x, dev_y, dev_d, sibling):
        pl.semaphore_signal(barrier, inc=1, device_id=dev, device_id_type=MESH)

    @pl.when(sec < n_sec - 1)
    def _():
        pl.semaphore_signal(barrier, inc=1, device_id=above, device_id_type=MESH)

    @pl.when(sec > 0)
    def _():
        pl.semaphore_signal(barrier, inc=1, device_id=below, device_id_type=MESH)

    step = LEARN_RATE * lag_ref[0].astype(jnp.float32)
    for i in range(4):
        s_t[i] = jnp.transpose(jnp.broadcast_to(s_in_ref[i : i + 1, :], (128, cols)))
    reps = ff // 128

    def row_scale(i, at):
        return jnp.concatenate([s_t[i, at, :]] * reps, axis=1)

    for c in l_in:
        c.wait()

    def predict_in(start):
        @pl.loop(0, cols // 2 // 32)
        def _(t):
            at = pl.ds(pl.multiple_of(start + t * 32, 32), 32)
            for k in range(2):
                p_in[0, at, k * ff : (k + 1) * ff] = predicted(
                    w_in[k, at, :], c_in[k, at, :], row_scale(k, at), row_scale(2 + k, at), step
                )

    hc = cols // 2
    hf = ff // 2
    lo, hi = pl.ds(0, hc), pl.ds(hc, hc)
    flo, fhi = pl.ds(0, hf), pl.ds(hf, hf)
    rlo, rhi = pl.ds(0, half_r), pl.ds(half_r, half_r)

    def spread(buf, first, second):
        to_x = [remote(buf.at[0, p], buf.at[1, p], dev_x) for p in (first, second)]
        to_y = [remote(buf.at[0, p], buf.at[2, p], dev_y) for p in (first, second)]
        on_y = remote(buf.at[1, first], buf.at[3, first], dev_y)
        on_x = remote(buf.at[2, second], buf.at[3, second], dev_x)
        return to_x, to_y, on_y, on_x

    a_x, a_y, a_on_y, a_on_x = spread(p_in, lo, hi)
    d_x, d_y, d_on_y, d_on_x = spread(p_out, flo, fhi)
    h_x, h_y, h_on_y, h_on_x = spread(h_all, rlo, rhi)
    g_x, g_y, g_on_y, g_on_x = spread(dgdu, rlo, rhi)

    predict_in(0)
    expect = 4 + jnp.where(sec > 0, 1, 0) + jnp.where(sec < n_sec - 1, 1, 0)
    pl.semaphore_wait(barrier, expect)
    a_x[0].start()
    a_y[0].start()
    predict_in(hc)
    a_y[1].start()
    a_x[1].start()

    for c in l_out:
        c.wait()
    sm, sv = s_out_ref[0:1, :], s_out_ref[1:2, :]

    @pl.loop(0, ff // 32)
    def _(t):
        at = pl.ds(pl.multiple_of(t * 32, 32), 32)
        p_out[0, at, :] = predicted(w_out[at, :], c_out[at, :], sm, sv, step)

    d_x[0].start()
    d_y[1].start()
    d_x[1].start()
    d_y[0].start()

    gain = gain_ref[...]

    def normalize(src, base):
        @pl.loop(0, rows // 16)
        def _(t):
            at = pl.ds(pl.multiple_of(t * 16, 16), 16)
            to = pl.ds(pl.multiple_of(base + t * 16, 16), 16)
            parts = [src[j, at, :].astype(jnp.float32) for j in range(n_dp)]
            total = functools.reduce(jnp.add, [p * p for p in parts])
            factor = lax.rsqrt(
                jnp.sum(total, axis=-1, keepdims=True) * (1.0 / (n_dp * cols)) + NORM_EPS
            )
            for j in range(n_dp):
                scaled = parts[j] * factor * gain[:, j * cols : (j + 1) * cols]
                nrm[j, to, :] = scaled.astype(jnp.bfloat16)

    for c in l_xb:
        c.wait()
    normalize(xb, rows)
    for c in l_xf:
        c.wait()
    normalize(xf, 0)
    for c in l_dy:
        c.wait()
    acc[...] = matmul(nrm[me], p_in[0])
    dh[...] = matmul_nt(dy[me], p_out[0])
    n_all[0] = nrm[me, rows:, :]
    dy_all[0] = dy[me]

    a_x[0].wait_recv()
    a_on_y.start()
    a_y[1].wait_recv()
    a_on_x.start()
    a_x[1].wait_recv()
    acc[...] += matmul(nrm[me_x], p_in[1])
    a_y[0].wait_recv()
    acc[...] += matmul(nrm[me_y], p_in[2])
    d_x[0].wait_recv()
    d_on_y.start()
    d_y[1].wait_recv()
    d_on_x.start()

    mine = pl.ds(pl.multiple_of(core * half_r, half_r), half_r)
    mine_b = pl.ds(pl.multiple_of(rows + core * half_r, half_r), half_r)
    share = []
    for slot, owner, dev in ((1, me_x, dev_x), (2, me_y, dev_y), (3, me_d, dev_d)):
        share.append((
            remote(dy.at[owner, mine], dy_all.at[slot, mine], dev),
            remote(dy_all.at[slot, mine], dy_all.at[slot, mine], sibling),
        ))
        share.append((
            remote(nrm.at[owner, mine_b], n_all.at[slot, mine], dev),
            remote(n_all.at[slot, mine], n_all.at[slot, mine], sibling),
        ))
    for c, _ in share:
        c.start()

    d_x[1].wait_recv()
    dh[...] += matmul_nt(dy[me_x], p_out[1])
    d_y[0].wait_recv()
    dh[...] += matmul_nt(dy[me_y], p_out[2])

    a_on_y.wait_recv()
    a_on_x.wait_recv()
    acc[...] += matmul(nrm[me_d], p_in[3])

    @pl.loop(0, rows // 32)
    def _(t):
        at = pl.ds(pl.multiple_of(t * 32, 32), 32)
        gate, up = acc[at, :ff], acc[at, ff:]
        hid[at, :] = (gate * jax.nn.sigmoid(gate) * up).astype(jnp.bfloat16)
        to = pl.ds(pl.multiple_of(rows + t * 32, 32), 32)
        gate, up = acc[to, :ff], acc[to, ff:]
        h_all[0, at, :] = (gate * jax.nn.sigmoid(gate) * up).astype(jnp.bfloat16)

    for c in (h_x[0], h_y[1], h_x[1], h_y[0]):
        c.start()
    hidden = hid[...]
    for slot in range(3):
        q_s[owners[slot]] = matmul(hidden, p_out[slot]).astype(jnp.bfloat16)
    d_on_y.wait_recv()
    d_on_x.wait_recv()
    dh[...] += matmul_nt(dy[me_d], p_out[3])

    @pl.loop(0, rows // 32)
    def _(t):
        at = pl.ds(pl.multiple_of(t * 32, 32), 32)
        to = pl.ds(pl.multiple_of(rows + t * 32, 32), 32)
        gate, up, grad = acc[to, :ff], acc[to, ff:], dh[at, :]
        sig = jax.nn.sigmoid(gate)
        dgdu[0, at, :ff] = (grad * up * sig * (1.0 + gate * (1.0 - sig))).astype(jnp.bfloat16)
        dgdu[0, at, ff:] = (grad * gate * sig).astype(jnp.bfloat16)

    for c in (g_x[0], g_y[1], g_x[1], g_y[0]):
        c.start()

    part = half_r // CHUNKS
    other = pl.multiple_of((1 - core) * half_r, half_r)
    own = pl.multiple_of(core * half_r, half_r)

    def swaps(src, dst):
        return [
            remote(
                src.at[:, pl.ds(pl.multiple_of(other + c * part, part), part)],
                dst.at[:, pl.ds(c * part, part)], sibling,
            )
            for c in range(CHUNKS)
        ]

    q_x, e_x = swaps(q_s, q_r), swaps(e_s, e_r)

    def moved(src, dst, dev):
        pairs = []
        for c in range(CHUNKS):
            at = pl.ds(pl.multiple_of(own + c * part, part), part)
            pairs.append((
                remote(src.at[pl.ds(c * part, part)], dst.at[at], dev),
                remote(dst.at[at], dst.at[at], sibling),
            ))
        return pairs

    y_m, dx_m = moved(y_s, y_b, above), moved(dx_s, dx_b, below)
    first, last = sec == 0, sec == n_sec - 1

    q_s[me_d] = matmul(hidden, p_out[3]).astype(jnp.bfloat16)
    for c in q_x:
        c.start()
    back = dgdu[0]
    for slot in range(4):
        e_s[owners[slot]] = matmul_nt(back, p_in[slot]).astype(jnp.bfloat16)
    for c in e_x:
        c.start()

    for c in range(CHUNKS):
        q_x[c].wait_recv()

        @pl.loop(0, part // 16)
        def _(t, c=c):
            at = pl.ds(pl.multiple_of(own + c * part + t * 16, 16), 16)
            near = pl.ds(pl.multiple_of(c * part + t * 16, 16), 16)
            for j in range(n_dp):
                total = q_s[j, at, :].astype(jnp.float32) + q_r[j, near, :].astype(jnp.float32)
                y_s[near, j * cols : (j + 1) * cols] = (
                    xf[j, at, :].astype(jnp.float32) + total
                ).astype(jnp.bfloat16)

        @pl.when(jnp.logical_not(last))
        def _(c=c):
            y_m[c][0].start()

    for c in range(CHUNKS):
        e_x[c].wait_recv()

        @pl.loop(0, part // 16)
        def _(t, c=c):
            at = pl.ds(pl.multiple_of(own + c * part + t * 16, 16), 16)
            near = pl.ds(pl.multiple_of(c * part + t * 16, 16), 16)
            xs = [xb[j, at, :].astype(jnp.float32) for j in range(n_dp)]
            total = functools.reduce(jnp.add, [p * p for p in xs])
            inv = 1.0 / (n_dp * cols)
            factor = lax.rsqrt(jnp.sum(total, axis=-1, keepdims=True) * inv + NORM_EPS)
            scaled = [
                gain[:, j * cols : (j + 1) * cols]
                * (e_s[j, at, :].astype(jnp.float32) + e_r[j, near, :].astype(jnp.float32))
                for j in range(n_dp)
            ]
            inner = functools.reduce(jnp.add, [s * x for s, x in zip(scaled, xs)])
            mean = jnp.sum(inner, axis=-1, keepdims=True) * inv
            tail = factor * factor * factor * mean
            for j in range(n_dp):
                dx_s[near, j * cols : (j + 1) * cols] = (
                    dy[j, at, :].astype(jnp.float32) + factor * scaled[j] - xs[j] * tail
                ).astype(jnp.bfloat16)

        @pl.when(jnp.logical_not(first))
        def _(c=c):
            dx_m[c][0].start()

    for c, on in share:
        c.wait_recv()
        on.start()
    h_x[0].wait_recv()
    h_on_y.start()
    h_y[1].wait_recv()
    h_on_x.start()
    g_x[0].wait_recv()
    g_on_y.start()
    g_y[1].wait_recv()
    g_on_x.start()

    @pl.when(first)
    def _():
        y_b[...] = jnp.zeros_like(y_b)

    @pl.when(jnp.logical_not(first))
    def _():
        for c, on in y_m:
            c.wait_recv()
            on.start()

    @pl.when(last)
    def _():
        dx_b[...] = jnp.zeros_like(dx_b)

    @pl.when(jnp.logical_not(last))
    def _():
        for c, on in dx_m:
            c.wait_recv()
            on.start()

    for _, on in share:
        on.wait_recv()
    h_x[1].wait_recv()
    h_y[0].wait_recv()
    h_on_y.wait_recv()
    h_on_x.wait_recv()
    tokens = n_dp * rows
    share_of = 1.0 / tokens
    g_out[...] = matmul_tn(h_all[...].reshape(tokens, ff), dy_all[...].reshape(tokens, cols))

    @pl.loop(0, ff // 32)
    def _(t):
        at = pl.ds(pl.multiple_of(t * 32, 32), 32)
        g_out[at, :] = updated(g_out[at, :] * share_of, c_out[at, :], sm, sv)

    store_ids = iter(range(store_sem.shape[0]))

    def store(src, dst):
        copy = pltpu.make_async_copy(src, dst, store_sem.at[next(store_ids)])
        copy.start()
        return copy

    stores = [store(g_out, u_out_out)]

    g_x[1].wait_recv()
    g_y[0].wait_recv()
    g_on_y.wait_recv()
    g_on_x.wait_recv()
    grad_in = matmul_tn(n_all[...].reshape(tokens, cols), dgdu[...].reshape(tokens, 2 * ff))
    for k in range(2):
        g_in[k] = grad_in[:, k * ff : (k + 1) * ff]

    @pl.loop(0, cols // 32)
    def _(t):
        at = pl.ds(pl.multiple_of(t * 32, 32), 32)
        for k in range(2):
            g_in[k, at, :] = updated(
                g_in[k, at, :] * share_of, c_in[k, at, :], row_scale(k, at), row_scale(2 + k, at)
            )

    stores.append(store(g_in, u_in_out))

    @pl.when(jnp.logical_not(first))
    def _():
        for c, on in y_m:
            on.wait_recv()
            on.wait_send()
        for c, _ in dx_m:
            c.wait_send()

    @pl.when(jnp.logical_not(last))
    def _():
        for c, on in dx_m:
            on.wait_recv()
            on.wait_send()
        for c, _ in y_m:
            c.wait_send()

    stores.append(store(y_b, y_out))
    stores.append(store(dx_b, dx_out))
    for group in ((a_x, a_y, a_on_y, a_on_x), (d_x, d_y, d_on_y, d_on_x),
                  (h_x, h_y, h_on_y, h_on_x), (g_x, g_y, g_on_y, g_on_x)):
        for c in (*group[0], *group[1], group[2], group[3]):
            c.wait_send()
    for c, on in share:
        c.wait_send()
        on.wait_send()
    for c in (*q_x, *e_x):
        c.wait_send()
    for c in stores:
        c.wait()


def tick(
    n_sec, n_dp,
    forward_input, backward_input, output_grad, norm_gain,
    in_weight, out_weight, in_codes, out_codes, in_scales, out_scales, section_lags,
):
    xf, xb, dy = forward_input[0], backward_input[0], output_grad[0]
    rows, width = xf.shape
    _, cols, ff = in_weight.shape[1:]
    half_r = rows // 2
    bf, f32 = jnp.bfloat16, jnp.float32
    vmem = pl.BlockSpec(memory_space=pltpu.VMEM)
    hbm = pl.BlockSpec(memory_space=pl.ANY)
    V = pltpu.VMEM
    wide = (n_dp, rows, cols)
    n_remote = 4 * 6 + 12 + 2 * CHUNKS + 4 * CHUNKS
    outs = pl.pallas_call(
        functools.partial(tick_kernel, n_sec),
        out_shape=(
            jax.ShapeDtypeStruct((rows, width), bf),
            jax.ShapeDtypeStruct((rows, width), bf),
            jax.ShapeDtypeStruct((2, cols, ff), f32),
            jax.ShapeDtypeStruct((ff, cols), f32),
        ),
        in_specs=[pl.BlockSpec(memory_space=pltpu.SMEM), vmem, vmem, vmem] + [hbm] * 7,
        out_specs=(hbm,) * 4,
        scratch_shapes=[
            V(wide, bf), V(wide, bf), V(wide, bf),
            V((2, cols, ff), f32), V((ff, cols), f32),
            V((2, cols, ff), jnp.int32), V((ff, cols), jnp.int32),
            V((4, cols, 128), f32),
            V((n_dp, cols, 2 * ff), bf), V((n_dp, ff, cols), bf),
            V((n_dp, 2 * rows, cols), bf),
            V((2 * rows, 2 * ff), f32), V((rows, ff), f32), V((rows, ff), bf),
            V((n_dp, rows, 2 * ff), bf), V((n_dp, rows, ff), bf), V(wide, bf), V(wide, bf),
            V(wide, bf), V((n_dp, half_r, cols), bf), V(wide, bf), V((n_dp, half_r, cols), bf),
            V((half_r, width), bf), V((half_r, width), bf), V((rows, width), bf), V((rows, width), bf),
            V((2, cols, ff), f32), V((ff, cols), f32),
            pltpu.SemaphoreType.DMA((4 + 3 * n_dp,)),
            pltpu.SemaphoreType.DMA((4,)),
            pltpu.SemaphoreType.DMA((n_remote,)),
            pltpu.SemaphoreType.DMA((n_remote,)),
        ],
        compiler_params=pltpu.CompilerParams(
            collective_id=0, has_side_effects=True, vmem_limit_bytes=56 * 1024 * 1024
        ),
    )(
        section_lags, norm_gain, in_scales[0].reshape(4, cols), out_scales[0].reshape(2, cols),
        xf, xb, dy, in_weight[0], out_weight[0], in_codes[0], out_codes[0],
    )
    return tuple(o[None] for o in outs)


def solution(mesh):
    in_specs = (
        P("section", "dp", None),
        P("section", "dp", None),
        P("section", "dp", None),
        P("section", None),
        P("section", None, "dp", "hid"),
        P("section", "hid", "dp"),
        P("section", None, "dp", "hid"),
        P("section", "hid", "dp"),
        P("section", None, None, "dp", "hid"),
        P("section", None, "hid", "dp"),
        P("section"),
    )
    out_specs = (
        P("section", "dp", None),
        P("section", "dp", None),
        P("section", None, "dp", "hid"),
        P("section", "hid", "dp"),
    )
    if (mesh.shape["dp"], mesh.shape["hid"]) == (4, 2):
        body = functools.partial(tick, mesh.shape["section"], mesh.shape["dp"])
    else:
        body = local
    return jax.shard_map(body, mesh=mesh, in_specs=in_specs, out_specs=out_specs, check_vma=False)
```

```python
import functools
import math

import jax
import jax.numpy as jnp
from jax import lax
from jax.experimental import pallas as pl
from jax.experimental.pallas import tpu as pltpu
from jax.sharding import PartitionSpec as P

QB = 256
STEP = 1000


BETA_ONE = 0.9
BETA_TWO = 0.999
ADAM_EPS = 1e-08
NORM_EPS = 1e-06
LEARN_RATE = 0.003
MESH = pl.DeviceIdType.MESH
CHUNKS = 2


def passed_along(block, axis, distance):
    devices = range(lax.axis_size(axis))
    route = [(i - distance, i) for i in devices if i - distance in devices]
    return lax.ppermute(block, axis, route)


def dequant(codes, first_scale, second_scale):
    high = (codes // 256).astype(jnp.float32)
    low = (codes % 256).astype(jnp.float32)
    moment_m = first_scale * (high - 63.0) / 63.0
    moment_v = jnp.square(second_scale * (0.25 + 0.75 * low / 255.0))
    return (moment_m, moment_v)


def direction(moment_m, moment_v, count):
    return (
        moment_m
        / (1.0 - BETA_ONE**count)
        / (jnp.sqrt(moment_v / (1.0 - BETA_TWO**count)) + ADAM_EPS)
    )


def normalize(inputs, gain):
    values = inputs.astype(jnp.float32)
    factor = lax.rsqrt(jnp.mean(values * values, axis=-1, keepdims=True) + NORM_EPS)
    return ((values * factor * gain).astype(jnp.bfloat16), factor, values)


def local(
    forward_input,
    backward_input,
    output_grad,
    norm_gain,
    in_weight,
    out_weight,
    in_codes,
    out_codes,
    in_scales,
    out_scales,
    section_lags,
):
    lag_value = section_lags[0].astype(jnp.float32)
    gain = norm_gain[0]
    m_in, v_in = dequant(
        in_codes[0],
        jnp.repeat(in_scales[0, 0], QB, axis=-1),
        jnp.repeat(in_scales[0, 1], QB, axis=-1),
    )
    m_out, v_out = dequant(
        out_codes[0],
        jnp.repeat(out_scales[0, 0], QB, axis=0),
        jnp.repeat(out_scales[0, 1], QB, axis=0),
    )
    pred_in = (in_weight[0] - LEARN_RATE * lag_value * direction(m_in, v_in, STEP - 1)).astype(
        jnp.bfloat16
    )
    pred_out = (out_weight[0] - LEARN_RATE * lag_value * direction(m_out, v_out, STEP - 1)).astype(
        jnp.bfloat16
    )
    full_in, full_out = (
        lax.all_gather(pred_in, "dp", axis=1, tiled=True),
        lax.all_gather(pred_out, "dp", axis=1, tiled=True),
    )
    normed, factor, values = normalize(forward_input[0], gain)
    gate_val = jnp.dot(normed, full_in[0], preferred_element_type=jnp.float32)
    up_val = jnp.dot(normed, full_in[1], preferred_element_type=jnp.float32)
    hidden = (gate_val * jax.nn.sigmoid(gate_val) * up_val).astype(jnp.bfloat16)
    partial_value = jnp.dot(hidden, full_out, preferred_element_type=jnp.float32)
    back_in, back_out = (full_in, full_out)
    out_cot = output_grad[0]
    normed_b, factor_b, values_b = normalize(backward_input[0], gain)
    gate_b = jnp.dot(normed_b, back_in[0], preferred_element_type=jnp.float32)
    up_b = jnp.dot(normed_b, back_in[1], preferred_element_type=jnp.float32)
    sig_b = jax.nn.sigmoid(gate_b)
    hidden_b = (gate_b * sig_b * up_b).astype(jnp.bfloat16)
    grad_h = jnp.dot(out_cot, back_out.T, preferred_element_type=jnp.float32)
    grad_gate = (grad_h * up_b * sig_b * (1.0 + gate_b * (1.0 - sig_b))).astype(jnp.bfloat16)
    grad_up = (grad_h * gate_b * sig_b).astype(jnp.bfloat16)
    grad_part = jnp.dot(grad_gate, back_in[0].T, preferred_element_type=jnp.float32) + jnp.dot(
        grad_up, back_in[1].T, preferred_element_type=jnp.float32
    )
    summed, grad_n = (
        lax.psum(partial_value.astype(jnp.bfloat16), "hid").astype(jnp.float32),
        lax.psum(grad_part.astype(jnp.bfloat16), "hid").astype(jnp.float32),
    )
    ahead = (values + summed).astype(jnp.bfloat16)
    next_rows = passed_along(ahead, "section", 1)
    scaled = gain * grad_n
    grad_x = (
        out_cot.astype(jnp.float32)
        + factor_b * scaled
        - values_b * factor_b**3 * jnp.mean(scaled * values_b, axis=-1, keepdims=True)
    )
    back_rows = passed_along(grad_x.astype(jnp.bfloat16), "section", -1)
    local_in = jnp.stack(
        [
            jnp.dot(normed_b.T, grad_gate, preferred_element_type=jnp.float32),
            jnp.dot(normed_b.T, grad_up, preferred_element_type=jnp.float32),
        ]
    )
    local_out = jnp.dot(hidden_b.T, out_cot, preferred_element_type=jnp.float32)
    sum_in, sum_out = (
        lax.psum_scatter(
            local_in.astype(jnp.bfloat16), "dp", scatter_dimension=1, tiled=True
        ).astype(jnp.float32),
        lax.psum_scatter(
            local_out.astype(jnp.bfloat16), "dp", scatter_dimension=1, tiled=True
        ).astype(jnp.float32),
    )
    rows_all = out_cot.shape[0] * lax.axis_size("dp")
    grad_in = sum_in / rows_all
    grad_out = sum_out / rows_all
    new_m_in = BETA_ONE * m_in + (1.0 - BETA_ONE) * grad_in
    new_v_in = BETA_TWO * v_in + (1.0 - BETA_TWO) * grad_in * grad_in
    new_m_out = BETA_ONE * m_out + (1.0 - BETA_ONE) * grad_out
    new_v_out = BETA_TWO * v_out + (1.0 - BETA_TWO) * grad_out * grad_out
    in_update = direction(new_m_in, new_v_in, STEP)
    out_update = direction(new_m_out, new_v_out, STEP)
    return (next_rows[None], back_rows[None], in_update[None], out_update[None])


def matmul(a, b):
    return jnp.dot(a, b, preferred_element_type=jnp.float32)


def matmul_nt(a, b):
    return lax.dot_general(a, b, (((1,), (1,)), ((), ())), preferred_element_type=jnp.float32)


def matmul_tn(a, b):
    return lax.dot_general(a, b, (((0,), (0,)), ((), ())), preferred_element_type=jnp.float32)


def moments(codes, first_scale, second_scale):
    high = (codes >> 8).astype(jnp.float32)
    low = (codes & 255).astype(jnp.float32)
    moment_m = first_scale * ((high - 63.0) * (1.0 / 63.0))
    root_v = second_scale * (0.25 + low * (0.75 / 255.0))
    return moment_m, root_v


def predicted(weight, codes, first_scale, second_scale, step):
    moment_m, root_v = moments(codes, first_scale, second_scale)
    count = STEP - 1
    top = moment_m * (step / (1.0 - BETA_ONE**count))
    bottom = root_v * (1.0 / math.sqrt(1.0 - BETA_TWO**count)) + ADAM_EPS
    return (weight - top / bottom).astype(jnp.bfloat16)


def decayed(codes, first_scale, second_scale):
    moment_m, root_v = moments(codes, first_scale, second_scale)
    keep_m = moment_m * (BETA_ONE / (1.0 - BETA_ONE**STEP))
    keep_v = root_v * root_v * (BETA_TWO / (1.0 - BETA_TWO**STEP))
    return keep_m, keep_v


def updated(total, keep_m, keep_v, tokens):
    part_m = (1.0 - BETA_ONE) / (1.0 - BETA_ONE**STEP) / tokens
    part_v = (1.0 - BETA_TWO) / (1.0 - BETA_TWO**STEP) / tokens**2
    new_v = keep_v + part_v * (total * total)
    return (keep_m + part_m * total) / (jnp.sqrt(new_v) + ADAM_EPS)


def tick_kernel(
    n_sec,
    lag_ref, gain_ref, s_in_ref, s_out_ref,
    xf_hbm, xb_hbm, dy_hbm, w_in_hbm, w_out_hbm, c_in_hbm, c_out_hbm,
    y_b, dx_b, g_out, g_in, m_in, v_in,
    xf, xb, dy, w_in, w_out, c_in, c_out, s_t,
    p_in, p_out, nrm, acc, dh, hid, dgdu, h_all, n_all, dy_all,
    q_s, q_r, e_s, e_r, y_s, dx_s,
    load_sem, send_sem, recv_sem,
):
    sec = lax.axis_index("section")
    me = lax.axis_index("dp")
    core = lax.axis_index("hid")
    n_dp, rows, cols = xf.shape
    ff = w_out.shape[0]
    half_r = rows // 2
    me_x = me + 1 - 2 * (me % 2)
    me_y = (me + 2) % 4
    me_d = 3 - me
    owners = (me, me_x, me_y, me_d)
    dev_x, dev_y, dev_d = ((sec, o, core) for o in owners[1:])
    sibling = (sec, me, 1 - core)
    above = (sec + 1, me, core)
    below = (sec - 1, me, core)

    ids = iter(range(send_sem.shape[0]))

    def remote(src, dst, dev):
        i = next(ids)
        return pltpu.make_async_remote_copy(
            src_ref=src, dst_ref=dst, send_sem=send_sem.at[i], recv_sem=recv_sem.at[i],
            device_id=dev, device_id_type=MESH,
        )

    lids = iter(range(load_sem.shape[0]))

    def load(src, dst):
        copy = pltpu.make_async_copy(src, dst, load_sem.at[next(lids)])
        copy.start()
        return copy

    def load_cols(src, dst):
        return [load(src.at[:, pl.ds(j * cols, cols)], dst.at[j]) for j in range(n_dp)]

    half_c = cols // 2
    l_in = [
        [
            load(src.at[:, pl.ds(at, half_c)], dst.at[:, pl.ds(at, half_c)])
            for src, dst in ((c_in_hbm, c_in), (w_in_hbm, w_in))
        ]
        for at in (0, half_c)
    ]
    l_out = [load(c_out_hbm, c_out), load(w_out_hbm, w_out)]
    l_xb = load_cols(xb_hbm, xb)
    l_xf = load_cols(xf_hbm, xf)
    l_dy = load_cols(dy_hbm, dy)

    barrier = pltpu.get_barrier_semaphore()
    for dev in (dev_x, dev_y, dev_d, sibling):
        pl.semaphore_signal(barrier, inc=1, device_id=dev, device_id_type=MESH)

    @pl.when(sec < n_sec - 1)
    def _():
        pl.semaphore_signal(barrier, inc=1, device_id=above, device_id_type=MESH)

    @pl.when(sec > 0)
    def _():
        pl.semaphore_signal(barrier, inc=1, device_id=below, device_id_type=MESH)

    step = LEARN_RATE * lag_ref[0].astype(jnp.float32)
    reps = ff // 128

    def row_scale(i, at):
        return jnp.concatenate([s_t[i, at, :]] * reps, axis=1)

    def predict_in(start):
        @pl.loop(0, cols // 2 // 32)
        def _(t):
            at = pl.ds(pl.multiple_of(start + t * 32, 32), 32)
            for k in range(2):
                p_in[0, at, k * ff : (k + 1) * ff] = predicted(
                    w_in[k, at, :], c_in[k, at, :], row_scale(k, at), row_scale(2 + k, at), step
                )

    hc = cols // 2
    hf = ff // 2
    lo, hi = pl.ds(0, hc), pl.ds(hc, hc)
    flo, fhi = pl.ds(0, hf), pl.ds(hf, hf)
    rlo, rhi = pl.ds(0, half_r), pl.ds(half_r, half_r)

    def spread(buf, first, second):
        to_x = [remote(buf.at[0, p], buf.at[1, p], dev_x) for p in (first, second)]
        to_y = [remote(buf.at[0, p], buf.at[2, p], dev_y) for p in (first, second)]
        on_y = remote(buf.at[1, first], buf.at[3, first], dev_y)
        on_x = remote(buf.at[2, second], buf.at[3, second], dev_x)
        return to_x, to_y, on_y, on_x

    a_x, a_y, a_on_y, a_on_x = spread(p_in, lo, hi)
    d_x, d_y, d_on_y, d_on_x = spread(p_out, flo, fhi)
    h_x, h_y, h_on_y, h_on_x = spread(h_all, rlo, rhi)
    g_x, g_y, g_on_y, g_on_x = spread(dgdu, rlo, rhi)

    mine = pl.ds(pl.multiple_of(core * half_r, half_r), half_r)
    mine_b = pl.ds(pl.multiple_of(rows + core * half_r, half_r), half_r)
    peers = ((1, me_x, dev_x), (2, me_y, dev_y), (3, me_d, dev_d))

    def columns(owner):
        return pl.ds(pl.multiple_of(owner * cols, cols), cols)

    share = [
        (
            remote(dy_hbm.at[mine, columns(owner)], dy_all.at[slot, mine], dev),
            remote(dy_all.at[slot, mine], dy_all.at[slot, mine], sibling),
        )
        for slot, owner, dev in peers
    ]
    share += [
        (
            remote(nrm.at[owner, mine_b], n_all.at[slot, mine], dev),
            remote(n_all.at[slot, mine], n_all.at[slot, mine], sibling),
        )
        for slot, owner, dev in peers
    ]

    expect = 4 + jnp.where(sec > 0, 1, 0) + jnp.where(sec < n_sec - 1, 1, 0)
    pl.semaphore_wait(barrier, expect)
    for c, _ in share[:3]:
        c.start()
    for i in range(4):
        s_t[i] = jnp.transpose(jnp.broadcast_to(s_in_ref[i], (128, cols)))
    for c in l_in[0]:
        c.wait()
    predict_in(0)
    a_x[0].start()
    a_y[0].start()
    for c in l_in[1]:
        c.wait()
    predict_in(hc)
    a_y[1].start()
    a_x[1].start()

    for c in l_out:
        c.wait()
    sm, sv = s_out_ref[0], s_out_ref[1]

    @pl.loop(0, ff // 32)
    def _(t):
        at = pl.ds(pl.multiple_of(t * 32, 32), 32)
        p_out[0, at, :] = predicted(w_out[at, :], c_out[at, :], sm, sv, step)

    d_x[0].start()
    d_y[1].start()
    d_x[1].start()
    d_y[0].start()

    gain = gain_ref[...]

    def normalize(src, base):
        @pl.loop(0, rows // 16)
        def _(t):
            at = pl.ds(pl.multiple_of(t * 16, 16), 16)
            to = pl.ds(pl.multiple_of(base + t * 16, 16), 16)
            parts = [src[j, at, :].astype(jnp.float32) for j in range(n_dp)]
            total = functools.reduce(jnp.add, [p * p for p in parts])
            factor = lax.rsqrt(
                jnp.sum(total, axis=-1, keepdims=True) * (1.0 / (n_dp * cols)) + NORM_EPS
            )
            for j in range(n_dp):
                scaled = parts[j] * factor * gain[:, j * cols : (j + 1) * cols]
                nrm[j, to, :] = scaled.astype(jnp.bfloat16)

    for c in l_xb:
        c.wait()
    normalize(xb, rows)
    for c in l_xf:
        c.wait()
    normalize(xf, 0)
    for c in l_dy:
        c.wait()
    acc[...] = matmul(nrm[me], p_in[0])
    dh[...] = matmul_nt(dy[me], p_out[0])
    n_all[0] = nrm[me, rows:, :]
    dy_all[0] = dy[me]

    @pl.loop(0, cols // 32)
    def _(t):
        at = pl.ds(pl.multiple_of(t * 32, 32), 32)
        for k in range(2):
            lanes = slice(k * ff, (k + 1) * ff)
            m_in[at, lanes], v_in[at, lanes] = decayed(
                c_in[k, at, :], row_scale(k, at), row_scale(2 + k, at)
            )

    a_x[0].wait_recv()
    a_on_y.start()
    a_y[1].wait_recv()
    a_on_x.start()
    a_x[1].wait_recv()
    acc[...] += matmul(nrm[me_x], p_in[1])
    a_y[0].wait_recv()
    acc[...] += matmul(nrm[me_y], p_in[2])
    d_x[0].wait_recv()
    d_on_y.start()
    d_y[1].wait_recv()
    d_on_x.start()

    for c, _ in share[3:]:
        c.start()

    d_x[1].wait_recv()
    dh[...] += matmul_nt(dy[me_x], p_out[1])
    d_y[0].wait_recv()
    dh[...] += matmul_nt(dy[me_y], p_out[2])

    a_on_y.wait_recv()
    a_on_x.wait_recv()
    acc[...] += matmul(nrm[me_d], p_in[3])

    @pl.loop(0, rows // 32)
    def _(t):
        at = pl.ds(pl.multiple_of(t * 32, 32), 32)
        gate, up = acc[at, :ff], acc[at, ff:]
        hid[at, :] = (gate * jax.nn.sigmoid(gate) * up).astype(jnp.bfloat16)
        to = pl.ds(pl.multiple_of(rows + t * 32, 32), 32)
        gate, up = acc[to, :ff], acc[to, ff:]
        h_all[0, at, :] = (gate * jax.nn.sigmoid(gate) * up).astype(jnp.bfloat16)

    for c in (h_x[0], h_y[1], h_x[1], h_y[0]):
        c.start()
    hidden = hid[...]
    for slot in range(3):
        q_s[owners[slot]] = matmul(hidden, p_out[slot]).astype(jnp.bfloat16)
    d_on_y.wait_recv()
    d_on_x.wait_recv()
    dh[...] += matmul_nt(dy[me_d], p_out[3])

    @pl.loop(0, rows // 32)
    def _(t):
        at = pl.ds(pl.multiple_of(t * 32, 32), 32)
        to = pl.ds(pl.multiple_of(rows + t * 32, 32), 32)
        gate, up, grad = acc[to, :ff], acc[to, ff:], dh[at, :]
        sig = jax.nn.sigmoid(gate)
        dgdu[0, at, :ff] = (grad * up * sig * (1.0 + gate * (1.0 - sig))).astype(jnp.bfloat16)
        dgdu[0, at, ff:] = (grad * gate * sig).astype(jnp.bfloat16)

    for c in (g_x[0], g_y[1], g_x[1], g_y[0]):
        c.start()

    part = half_r // CHUNKS
    other = pl.multiple_of((1 - core) * half_r, half_r)
    own = pl.multiple_of(core * half_r, half_r)

    def swaps(src, dst):
        return [
            remote(
                src.at[:, pl.ds(pl.multiple_of(other + c * part, part), part)],
                dst.at[:, pl.ds(c * part, part)], sibling,
            )
            for c in range(CHUNKS)
        ]

    q_x, e_x = swaps(q_s, q_r), swaps(e_s, e_r)

    def moved(src, dst, dev):
        pairs = []
        for c in range(CHUNKS):
            at = pl.ds(pl.multiple_of(own + c * part, part), part)
            pairs.append((
                remote(src.at[pl.ds(c * part, part)], dst.at[at], dev),
                remote(dst.at[at], dst.at[at], sibling),
            ))
        return pairs

    y_m, dx_m = moved(y_s, y_b, above), moved(dx_s, dx_b, below)
    first, last = sec == 0, sec == n_sec - 1

    q_s[me_d] = matmul(hidden, p_out[3]).astype(jnp.bfloat16)
    for c in q_x:
        c.start()
    back = dgdu[0]
    for slot in range(4):
        e_s[owners[slot]] = matmul_nt(back, p_in[slot]).astype(jnp.bfloat16)
    for c in e_x:
        c.start()

    for c in range(CHUNKS):
        q_x[c].wait_recv()

        @pl.loop(0, part // 16)
        def _(t, c=c):
            at = pl.ds(pl.multiple_of(own + c * part + t * 16, 16), 16)
            near = pl.ds(pl.multiple_of(c * part + t * 16, 16), 16)
            for j in range(n_dp):
                total = q_s[j, at, :].astype(jnp.float32) + q_r[j, near, :].astype(jnp.float32)
                y_s[near, j * cols : (j + 1) * cols] = (
                    xf[j, at, :].astype(jnp.float32) + total
                ).astype(jnp.bfloat16)

        @pl.when(jnp.logical_not(last))
        def _(c=c):
            y_m[c][0].start()

    for c in range(CHUNKS):
        e_x[c].wait_recv()

        @pl.loop(0, part // 16)
        def _(t, c=c):
            at = pl.ds(pl.multiple_of(own + c * part + t * 16, 16), 16)
            near = pl.ds(pl.multiple_of(c * part + t * 16, 16), 16)
            xs = [xb[j, at, :].astype(jnp.float32) for j in range(n_dp)]
            total = functools.reduce(jnp.add, [p * p for p in xs])
            inv = 1.0 / (n_dp * cols)
            factor = lax.rsqrt(jnp.sum(total, axis=-1, keepdims=True) * inv + NORM_EPS)
            scaled = [
                gain[:, j * cols : (j + 1) * cols]
                * (e_s[j, at, :].astype(jnp.float32) + e_r[j, near, :].astype(jnp.float32))
                for j in range(n_dp)
            ]
            inner = functools.reduce(jnp.add, [s * x for s, x in zip(scaled, xs)])
            mean = jnp.sum(inner, axis=-1, keepdims=True) * inv
            tail = factor * factor * factor * mean
            for j in range(n_dp):
                dx_s[near, j * cols : (j + 1) * cols] = (
                    dy[j, at, :].astype(jnp.float32) + factor * scaled[j] - xs[j] * tail
                ).astype(jnp.bfloat16)

        @pl.when(jnp.logical_not(first))
        def _(c=c):
            dx_m[c][0].start()

    for c, on in share:
        c.wait_recv()
        on.start()
    h_x[0].wait_recv()
    h_on_y.start()
    h_y[1].wait_recv()
    h_on_x.start()
    g_x[0].wait_recv()
    g_on_y.start()
    g_y[1].wait_recv()
    g_on_x.start()

    @pl.when(first)
    def _():
        y_b[...] = jnp.zeros_like(y_b)

    @pl.when(jnp.logical_not(first))
    def _():
        for c, on in y_m:
            c.wait_recv()
            on.start()

    @pl.when(last)
    def _():
        dx_b[...] = jnp.zeros_like(dx_b)

    @pl.when(jnp.logical_not(last))
    def _():
        for c, on in dx_m:
            c.wait_recv()
            on.start()

    for _, on in share:
        on.wait_recv()
    h_x[1].wait_recv()
    h_y[0].wait_recv()
    h_on_y.wait_recv()
    h_on_x.wait_recv()
    tokens = n_dp * rows
    g_out[...] = matmul_tn(h_all[...].reshape(tokens, ff), dy_all[...].reshape(tokens, cols))

    @pl.loop(0, ff // 32)
    def _(t):
        at = pl.ds(pl.multiple_of(t * 32, 32), 32)
        keep_m, keep_v = decayed(c_out[at, :], sm, sv)
        g_out[at, :] = updated(g_out[at, :], keep_m, keep_v, tokens)

    g_x[1].wait_recv()
    g_y[0].wait_recv()
    near = 3 * rows
    g_in[...] = matmul_tn(n_all[:3].reshape(near, cols), dgdu[:3].reshape(near, 2 * ff))
    g_on_y.wait_recv()
    g_on_x.wait_recv()
    g_in[...] += matmul_tn(n_all[3], dgdu[3])

    @pl.when(jnp.logical_not(first))
    def _():
        for c, on in y_m:
            on.wait_recv()
            on.wait_send()
        for c, _ in dx_m:
            c.wait_send()

    @pl.when(jnp.logical_not(last))
    def _():
        for c, on in dx_m:
            on.wait_recv()
            on.wait_send()
        for c, _ in y_m:
            c.wait_send()

    for group in ((a_x, a_y, a_on_y, a_on_x), (d_x, d_y, d_on_y, d_on_x),
                  (h_x, h_y, h_on_y, h_on_x), (g_x, g_y, g_on_y, g_on_x)):
        for c in (*group[0], *group[1], group[2], group[3]):
            c.wait_send()
    for c, on in share:
        c.wait_send()
        on.wait_send()
    for c in (*q_x, *e_x):
        c.wait_send()


def finish_kernel(
    tokens, y_b, dx_b, u_out, g_in, m_in, v_in,
    y_hbm, dx_hbm, u_in_hbm, u_out_hbm, u_in, sem,
):
    _, cols, ff = u_in.shape
    copies = [
        pltpu.make_async_copy(src, dst, sem.at[i])
        for i, (src, dst) in enumerate(((y_b, y_hbm), (dx_b, dx_hbm), (u_out, u_out_hbm)))
    ]
    for c in copies:
        c.start()
    pieces = 2
    tall = cols // pieces
    for piece in range(pieces):
        @pl.loop(0, tall // 32)
        def _(t, piece=piece):
            at = pl.ds(pl.multiple_of(piece * tall + t * 32, 32), 32)
            for k in range(2):
                lanes = slice(k * ff, (k + 1) * ff)
                u_in[k, at, :] = updated(g_in[at, lanes], m_in[at, lanes], v_in[at, lanes], tokens)

        at = pl.ds(piece * tall, tall)
        c = pltpu.make_async_copy(u_in.at[:, at], u_in_hbm.at[:, at], sem.at[3 + piece])
        c.start()
        copies.append(c)
    for c in copies:
        c.wait()


def tick(
    n_sec, n_dp,
    forward_input, backward_input, output_grad, norm_gain,
    in_weight, out_weight, in_codes, out_codes, in_scales, out_scales, section_lags,
):
    xf, xb, dy = forward_input[0], backward_input[0], output_grad[0]
    rows, width = xf.shape
    _, cols, ff = in_weight.shape[1:]
    half_r = rows // 2
    bf, f32 = jnp.bfloat16, jnp.float32
    vmem = pl.BlockSpec(memory_space=pltpu.VMEM)
    hbm = pl.BlockSpec(memory_space=pltpu.HBM)
    V = pltpu.VMEM
    wide = (n_dp, rows, cols)
    n_remote = 4 * 6 + 12 + 2 * CHUNKS + 4 * CHUNKS
    held = pl.pallas_call(
        functools.partial(tick_kernel, n_sec),
        out_shape=(
            V((rows, width), bf),
            V((rows, width), bf),
            V((ff, cols), f32),
            V((cols, 2 * ff), f32),
            V((cols, 2 * ff), f32),
            V((cols, 2 * ff), f32),
        ),
        in_specs=[pl.BlockSpec(memory_space=pltpu.SMEM), vmem, vmem, vmem] + [hbm] * 7,
        out_specs=(vmem,) * 6,
        scratch_shapes=[
            V(wide, bf), V(wide, bf), V(wide, bf),
            V((2, cols, ff), f32), V((ff, cols), f32),
            V((2, cols, ff), jnp.int32), V((ff, cols), jnp.int32),
            V((4, cols, 128), f32),
            V((n_dp, cols, 2 * ff), bf), V((n_dp, ff, cols), bf),
            V((n_dp, 2 * rows, cols), bf),
            V((2 * rows, 2 * ff), f32), V((rows, ff), f32), V((rows, ff), bf),
            V((n_dp, rows, 2 * ff), bf), V((n_dp, rows, ff), bf), V(wide, bf), V(wide, bf),
            V(wide, bf), V((n_dp, half_r, cols), bf), V(wide, bf), V((n_dp, half_r, cols), bf),
            V((half_r, width), bf), V((half_r, width), bf),
            pltpu.SemaphoreType.DMA((6 + 3 * n_dp,)),
            pltpu.SemaphoreType.DMA((n_remote,)),
            pltpu.SemaphoreType.DMA((n_remote,)),
        ],
        compiler_params=pltpu.CompilerParams(
            collective_id=0, has_side_effects=True, vmem_limit_bytes=61200000
        ),
    )(
        section_lags, norm_gain, jnp.swapaxes(in_scales[0], 2, 3).reshape(4, 1, cols), out_scales[0],
        xf, xb, dy, in_weight[0], out_weight[0], in_codes[0], out_codes[0],
    )
    outs = pl.pallas_call(
        functools.partial(finish_kernel, rows * n_dp),
        out_shape=(
            jax.ShapeDtypeStruct((rows, width), bf),
            jax.ShapeDtypeStruct((rows, width), bf),
            jax.ShapeDtypeStruct((2, cols, ff), f32),
            jax.ShapeDtypeStruct((ff, cols), f32),
        ),
        in_specs=[vmem] * 6,
        out_specs=(hbm,) * 4,
        scratch_shapes=[V((2, cols, ff), f32), pltpu.SemaphoreType.DMA((5,))],
        compiler_params=pltpu.CompilerParams(vmem_limit_bytes=16 * 1024 * 1024),
    )(*held)
    return tuple(o[None] for o in outs)


def solution(mesh):
    in_specs = (
        P("section", "dp", None),
        P("section", "dp", None),
        P("section", "dp", None),
        P("section", None),
        P("section", None, "dp", "hid"),
        P("section", "hid", "dp"),
        P("section", None, "dp", "hid"),
        P("section", "hid", "dp"),
        P("section", None, None, "dp", "hid"),
        P("section", None, "hid", "dp"),
        P("section"),
    )
    out_specs = (
        P("section", "dp", None),
        P("section", "dp", None),
        P("section", None, "dp", "hid"),
        P("section", "hid", "dp"),
    )
    if (mesh.shape["dp"], mesh.shape["hid"]) == (4, 2):
        body = functools.partial(tick, mesh.shape["section"], mesh.shape["dp"])
    else:
        body = local
    return jax.shard_map(body, mesh=mesh, in_specs=in_specs, out_specs=out_specs, check_vma=False)
```

```python
import functools
import math

import jax
import jax.numpy as jnp
from jax import lax
from jax.experimental import pallas as pl
from jax.experimental.pallas import tpu as pltpu
from jax.sharding import PartitionSpec as P

QB = 256
STEP = 1000


BETA_ONE = 0.9
BETA_TWO = 0.999
ADAM_EPS = 1e-08
NORM_EPS = 1e-06
LEARN_RATE = 0.003
MESH = pl.DeviceIdType.MESH
CHUNKS = 2


def passed_along(block, axis, distance):
    devices = range(lax.axis_size(axis))
    route = [(i - distance, i) for i in devices if i - distance in devices]
    return lax.ppermute(block, axis, route)


def dequant(codes, first_scale, second_scale):
    high = (codes // 256).astype(jnp.float32)
    low = (codes % 256).astype(jnp.float32)
    moment_m = first_scale * (high - 63.0) / 63.0
    moment_v = jnp.square(second_scale * (0.25 + 0.75 * low / 255.0))
    return (moment_m, moment_v)


def direction(moment_m, moment_v, count):
    return (
        moment_m
        / (1.0 - BETA_ONE**count)
        / (jnp.sqrt(moment_v / (1.0 - BETA_TWO**count)) + ADAM_EPS)
    )


def normalize(inputs, gain):
    values = inputs.astype(jnp.float32)
    factor = lax.rsqrt(jnp.mean(values * values, axis=-1, keepdims=True) + NORM_EPS)
    return ((values * factor * gain).astype(jnp.bfloat16), factor, values)


def local(
    forward_input,
    backward_input,
    output_grad,
    norm_gain,
    in_weight,
    out_weight,
    in_codes,
    out_codes,
    in_scales,
    out_scales,
    section_lags,
):
    lag_value = section_lags[0].astype(jnp.float32)
    gain = norm_gain[0]
    m_in, v_in = dequant(
        in_codes[0],
        jnp.repeat(in_scales[0, 0], QB, axis=-1),
        jnp.repeat(in_scales[0, 1], QB, axis=-1),
    )
    m_out, v_out = dequant(
        out_codes[0],
        jnp.repeat(out_scales[0, 0], QB, axis=0),
        jnp.repeat(out_scales[0, 1], QB, axis=0),
    )
    pred_in = (in_weight[0] - LEARN_RATE * lag_value * direction(m_in, v_in, STEP - 1)).astype(
        jnp.bfloat16
    )
    pred_out = (out_weight[0] - LEARN_RATE * lag_value * direction(m_out, v_out, STEP - 1)).astype(
        jnp.bfloat16
    )
    full_in, full_out = (
        lax.all_gather(pred_in, "dp", axis=1, tiled=True),
        lax.all_gather(pred_out, "dp", axis=1, tiled=True),
    )
    normed, factor, values = normalize(forward_input[0], gain)
    gate_val = jnp.dot(normed, full_in[0], preferred_element_type=jnp.float32)
    up_val = jnp.dot(normed, full_in[1], preferred_element_type=jnp.float32)
    hidden = (gate_val * jax.nn.sigmoid(gate_val) * up_val).astype(jnp.bfloat16)
    partial_value = jnp.dot(hidden, full_out, preferred_element_type=jnp.float32)
    back_in, back_out = (full_in, full_out)
    out_cot = output_grad[0]
    normed_b, factor_b, values_b = normalize(backward_input[0], gain)
    gate_b = jnp.dot(normed_b, back_in[0], preferred_element_type=jnp.float32)
    up_b = jnp.dot(normed_b, back_in[1], preferred_element_type=jnp.float32)
    sig_b = jax.nn.sigmoid(gate_b)
    hidden_b = (gate_b * sig_b * up_b).astype(jnp.bfloat16)
    grad_h = jnp.dot(out_cot, back_out.T, preferred_element_type=jnp.float32)
    grad_gate = (grad_h * up_b * sig_b * (1.0 + gate_b * (1.0 - sig_b))).astype(jnp.bfloat16)
    grad_up = (grad_h * gate_b * sig_b).astype(jnp.bfloat16)
    grad_part = jnp.dot(grad_gate, back_in[0].T, preferred_element_type=jnp.float32) + jnp.dot(
        grad_up, back_in[1].T, preferred_element_type=jnp.float32
    )
    summed, grad_n = (
        lax.psum(partial_value.astype(jnp.bfloat16), "hid").astype(jnp.float32),
        lax.psum(grad_part.astype(jnp.bfloat16), "hid").astype(jnp.float32),
    )
    ahead = (values + summed).astype(jnp.bfloat16)
    next_rows = passed_along(ahead, "section", 1)
    scaled = gain * grad_n
    grad_x = (
        out_cot.astype(jnp.float32)
        + factor_b * scaled
        - values_b * factor_b**3 * jnp.mean(scaled * values_b, axis=-1, keepdims=True)
    )
    back_rows = passed_along(grad_x.astype(jnp.bfloat16), "section", -1)
    local_in = jnp.stack(
        [
            jnp.dot(normed_b.T, grad_gate, preferred_element_type=jnp.float32),
            jnp.dot(normed_b.T, grad_up, preferred_element_type=jnp.float32),
        ]
    )
    local_out = jnp.dot(hidden_b.T, out_cot, preferred_element_type=jnp.float32)
    sum_in, sum_out = (
        lax.psum_scatter(
            local_in.astype(jnp.bfloat16), "dp", scatter_dimension=1, tiled=True
        ).astype(jnp.float32),
        lax.psum_scatter(
            local_out.astype(jnp.bfloat16), "dp", scatter_dimension=1, tiled=True
        ).astype(jnp.float32),
    )
    rows_all = out_cot.shape[0] * lax.axis_size("dp")
    grad_in = sum_in / rows_all
    grad_out = sum_out / rows_all
    new_m_in = BETA_ONE * m_in + (1.0 - BETA_ONE) * grad_in
    new_v_in = BETA_TWO * v_in + (1.0 - BETA_TWO) * grad_in * grad_in
    new_m_out = BETA_ONE * m_out + (1.0 - BETA_ONE) * grad_out
    new_v_out = BETA_TWO * v_out + (1.0 - BETA_TWO) * grad_out * grad_out
    in_update = direction(new_m_in, new_v_in, STEP)
    out_update = direction(new_m_out, new_v_out, STEP)
    return (next_rows[None], back_rows[None], in_update[None], out_update[None])


def matmul(a, b):
    return jnp.dot(a, b, preferred_element_type=jnp.float32)


def matmul_nt(a, b):
    return lax.dot_general(a, b, (((1,), (1,)), ((), ())), preferred_element_type=jnp.float32)


def matmul_tn(a, b):
    return lax.dot_general(a, b, (((0,), (0,)), ((), ())), preferred_element_type=jnp.float32)


def moments(codes, first_scale, second_scale):
    high = (codes >> 8).astype(jnp.float32)
    low = (codes & 255).astype(jnp.float32)
    moment_m = first_scale * ((high - 63.0) * (1.0 / 63.0))
    root_v = second_scale * (0.25 + low * (0.75 / 255.0))
    return moment_m, root_v


def predicted(weight, codes, first_scale, second_scale, step):
    moment_m, root_v = moments(codes, first_scale, second_scale)
    count = STEP - 1
    top = moment_m * (step / (1.0 - BETA_ONE**count))
    bottom = root_v * (1.0 / math.sqrt(1.0 - BETA_TWO**count)) + ADAM_EPS
    return (weight - top / bottom).astype(jnp.bfloat16)


def decayed(codes, first_scale, second_scale):
    moment_m, root_v = moments(codes, first_scale, second_scale)
    keep_m = moment_m * (BETA_ONE / (1.0 - BETA_ONE**STEP))
    keep_v = root_v * root_v * (BETA_TWO / (1.0 - BETA_TWO**STEP))
    return keep_m, keep_v


def updated(total, keep_m, keep_v, tokens):
    part_m = (1.0 - BETA_ONE) / (1.0 - BETA_ONE**STEP) / tokens
    part_v = (1.0 - BETA_TWO) / (1.0 - BETA_TWO**STEP) / tokens**2
    new_v = keep_v + part_v * (total * total)
    return (keep_m + part_m * total) / (jnp.sqrt(new_v) + ADAM_EPS)


def tick_kernel(
    n_sec,
    lag_ref, gain_ref, s_in_ref, s_out_ref,
    xf_hbm, xb_hbm, dy_hbm, w_in_hbm, w_out_hbm, c_in_hbm, c_out_hbm,
    y_b, dx_b, g_out, g_in, m_in, v_in,
    xf, xb, dy, w_in, w_out, c_in, c_out, s_t,
    p_in, p_out, nrm, acc, dh, hid, dgdu, h_all, n_all, dy_all,
    q_s, q_r, e_s, e_r, y_s, dx_s,
    load_sem, send_sem, recv_sem,
):
    sec = lax.axis_index("section")
    me = lax.axis_index("dp")
    core = lax.axis_index("hid")
    n_dp, rows, cols = xf.shape
    ff = w_out.shape[0]
    half_r = rows // 2
    me_x = me + 1 - 2 * (me % 2)
    me_y = (me + 2) % 4
    me_d = 3 - me
    owners = (me, me_x, me_y, me_d)
    dev_x, dev_y, dev_d = ((sec, o, core) for o in owners[1:])
    sibling = (sec, me, 1 - core)
    above = (sec + 1, me, core)
    below = (sec - 1, me, core)

    ids = iter(range(send_sem.shape[0]))

    def remote(src, dst, dev):
        i = next(ids)
        return pltpu.make_async_remote_copy(
            src_ref=src, dst_ref=dst, send_sem=send_sem.at[i], recv_sem=recv_sem.at[i],
            device_id=dev, device_id_type=MESH,
        )

    lids = iter(range(load_sem.shape[0]))

    def load(src, dst):
        copy = pltpu.make_async_copy(src, dst, load_sem.at[next(lids)])
        copy.start()
        return copy

    def load_cols(src, dst):
        return [load(src.at[:, pl.ds(j * cols, cols)], dst.at[j]) for j in range(n_dp)]

    half_c = cols // 2
    l_in = [
        [
            load(src.at[:, pl.ds(at, half_c)], dst.at[:, pl.ds(at, half_c)])
            for src, dst in ((c_in_hbm, c_in), (w_in_hbm, w_in))
        ]
        for at in (0, half_c)
    ]
    l_out = [load(c_out_hbm, c_out), load(w_out_hbm, w_out)]
    l_xb = load_cols(xb_hbm, xb)
    l_xf = load_cols(xf_hbm, xf)
    l_dy = load_cols(dy_hbm, dy)

    barrier = pltpu.get_barrier_semaphore()
    for dev in (dev_x, dev_y, dev_d, sibling):
        pl.semaphore_signal(barrier, inc=1, device_id=dev, device_id_type=MESH)

    @pl.when(sec < n_sec - 1)
    def _():
        pl.semaphore_signal(barrier, inc=1, device_id=above, device_id_type=MESH)

    @pl.when(sec > 0)
    def _():
        pl.semaphore_signal(barrier, inc=1, device_id=below, device_id_type=MESH)

    step = LEARN_RATE * lag_ref[0].astype(jnp.float32)
    reps = ff // 128

    def row_scale(i, at):
        return jnp.concatenate([s_t[i, at, :]] * reps, axis=1)

    def predict_in(start):
        @pl.loop(0, cols // 2 // 32)
        def _(t):
            at = pl.ds(pl.multiple_of(start + t * 32, 32), 32)
            for k in range(2):
                p_in[0, at, k * ff : (k + 1) * ff] = predicted(
                    w_in[k, at, :], c_in[k, at, :], row_scale(k, at), row_scale(2 + k, at), step
                )

    hc = cols // 2
    hf = ff // 2
    lo, hi = pl.ds(0, hc), pl.ds(hc, hc)
    flo, fhi = pl.ds(0, hf), pl.ds(hf, hf)
    rlo, rhi = pl.ds(0, half_r), pl.ds(half_r, half_r)

    def spread(buf, first, second):
        to_x = [remote(buf.at[0, p], buf.at[1, p], dev_x) for p in (first, second)]
        to_y = [remote(buf.at[0, p], buf.at[2, p], dev_y) for p in (first, second)]
        on_y = remote(buf.at[1, first], buf.at[3, first], dev_y)
        on_x = remote(buf.at[2, second], buf.at[3, second], dev_x)
        return to_x, to_y, on_y, on_x

    a_x, a_y, a_on_y, a_on_x = spread(p_in, lo, hi)
    d_x, d_y, d_on_y, d_on_x = spread(p_out, flo, fhi)
    h_x, h_y, h_on_y, h_on_x = spread(h_all, rlo, rhi)
    g_x, g_y, g_on_y, g_on_x = spread(dgdu, rlo, rhi)

    mine = pl.ds(pl.multiple_of(core * half_r, half_r), half_r)
    mine_b = pl.ds(pl.multiple_of(rows + core * half_r, half_r), half_r)
    peers = ((1, me_x, dev_x), (2, me_y, dev_y), (3, me_d, dev_d))

    def columns(owner):
        return pl.ds(pl.multiple_of(owner * cols, cols), cols)

    share = [
        (
            remote(dy_hbm.at[mine, columns(owner)], dy_all.at[slot, mine], dev),
            remote(dy_all.at[slot, mine], dy_all.at[slot, mine], sibling),
        )
        for slot, owner, dev in peers
    ]
    share += [
        (
            remote(nrm.at[owner, mine_b], n_all.at[slot, mine], dev),
            remote(n_all.at[slot, mine], n_all.at[slot, mine], sibling),
        )
        for slot, owner, dev in peers
    ]

    expect = 4 + jnp.where(sec > 0, 1, 0) + jnp.where(sec < n_sec - 1, 1, 0)
    pl.semaphore_wait(barrier, expect)
    for i in range(4):
        s_t[i] = jnp.transpose(jnp.broadcast_to(s_in_ref[i], (128, cols)))
    for c in l_in[0]:
        c.wait()
    predict_in(0)
    a_x[0].start()
    a_y[0].start()
    for c in l_in[1]:
        c.wait()
    predict_in(hc)
    a_y[1].start()
    a_x[1].start()

    for c in l_out:
        c.wait()
    sm, sv = s_out_ref[0], s_out_ref[1]

    @pl.loop(0, ff // 32)
    def _(t):
        at = pl.ds(pl.multiple_of(t * 32, 32), 32)
        p_out[0, at, :] = predicted(w_out[at, :], c_out[at, :], sm, sv, step)

    d_x[0].start()
    d_y[1].start()
    d_x[1].start()
    d_y[0].start()

    gain = gain_ref[...]

    def normalize(src, base):
        @pl.loop(0, rows // 16)
        def _(t):
            at = pl.ds(pl.multiple_of(t * 16, 16), 16)
            to = pl.ds(pl.multiple_of(base + t * 16, 16), 16)
            parts = [src[j, at, :].astype(jnp.float32) for j in range(n_dp)]
            total = functools.reduce(jnp.add, [p * p for p in parts])
            factor = lax.rsqrt(
                jnp.sum(total, axis=-1, keepdims=True) * (1.0 / (n_dp * cols)) + NORM_EPS
            )
            for j in range(n_dp):
                scaled = parts[j] * factor * gain[:, j * cols : (j + 1) * cols]
                nrm[j, to, :] = scaled.astype(jnp.bfloat16)

    for c in l_xb:
        c.wait()
    normalize(xb, rows)
    for c in l_xf:
        c.wait()
    normalize(xf, 0)
    for c in l_dy:
        c.wait()
    acc[...] = matmul(nrm[me], p_in[0])
    dh[...] = matmul_nt(dy[me], p_out[0])
    n_all[0] = nrm[me, rows:, :]
    dy_all[0] = dy[me]

    @pl.loop(0, cols // 32)
    def _(t):
        at = pl.ds(pl.multiple_of(t * 32, 32), 32)
        for k in range(2):
            lanes = slice(k * ff, (k + 1) * ff)
            m_in[at, lanes], v_in[at, lanes] = decayed(
                c_in[k, at, :], row_scale(k, at), row_scale(2 + k, at)
            )

    a_x[0].wait_recv()
    a_on_y.start()
    a_y[1].wait_recv()
    a_on_x.start()
    a_x[1].wait_recv()
    acc[...] += matmul(nrm[me_x], p_in[1])
    a_y[0].wait_recv()
    acc[...] += matmul(nrm[me_y], p_in[2])
    d_x[0].wait_recv()
    d_on_y.start()
    d_y[1].wait_recv()
    d_on_x.start()

    for c, _ in share[:3]:
        c.start()
    for c, _ in share[3:]:
        c.start()

    d_x[1].wait_recv()
    dh[...] += matmul_nt(dy[me_x], p_out[1])
    d_y[0].wait_recv()
    dh[...] += matmul_nt(dy[me_y], p_out[2])

    a_on_y.wait_recv()
    a_on_x.wait_recv()
    acc[...] += matmul(nrm[me_d], p_in[3])

    @pl.loop(0, rows // 32)
    def _(t):
        at = pl.ds(pl.multiple_of(t * 32, 32), 32)
        gate, up = acc[at, :ff], acc[at, ff:]
        hid[at, :] = (gate * jax.nn.sigmoid(gate) * up).astype(jnp.bfloat16)
        to = pl.ds(pl.multiple_of(rows + t * 32, 32), 32)
        gate, up = acc[to, :ff], acc[to, ff:]
        h_all[0, at, :] = (gate * jax.nn.sigmoid(gate) * up).astype(jnp.bfloat16)

    for c in (h_x[0], h_y[1], h_x[1], h_y[0]):
        c.start()
    hidden = hid[...]
    for slot in range(3):
        q_s[owners[slot]] = matmul(hidden, p_out[slot]).astype(jnp.bfloat16)
    d_on_y.wait_recv()
    d_on_x.wait_recv()
    dh[...] += matmul_nt(dy[me_d], p_out[3])

    @pl.loop(0, rows // 32)
    def _(t):
        at = pl.ds(pl.multiple_of(t * 32, 32), 32)
        to = pl.ds(pl.multiple_of(rows + t * 32, 32), 32)
        gate, up, grad = acc[to, :ff], acc[to, ff:], dh[at, :]
        sig = jax.nn.sigmoid(gate)
        dgdu[0, at, :ff] = (grad * up * sig * (1.0 + gate * (1.0 - sig))).astype(jnp.bfloat16)
        dgdu[0, at, ff:] = (grad * gate * sig).astype(jnp.bfloat16)

    for c in (g_x[0], g_y[1], g_x[1], g_y[0]):
        c.start()

    part = half_r // CHUNKS
    other = pl.multiple_of((1 - core) * half_r, half_r)
    own = pl.multiple_of(core * half_r, half_r)

    def swaps(src, dst):
        return [
            remote(
                src.at[:, pl.ds(pl.multiple_of(other + c * part, part), part)],
                dst.at[:, pl.ds(c * part, part)], sibling,
            )
            for c in range(CHUNKS)
        ]

    q_x, e_x = swaps(q_s, q_r), swaps(e_s, e_r)

    def moved(src, dst, dev):
        pairs = []
        for c in range(CHUNKS):
            at = pl.ds(pl.multiple_of(own + c * part, part), part)
            pairs.append((
                remote(src.at[pl.ds(c * part, part)], dst.at[at], dev),
                remote(dst.at[at], dst.at[at], sibling),
            ))
        return pairs

    y_m, dx_m = moved(y_s, y_b, above), moved(dx_s, dx_b, below)
    first, last = sec == 0, sec == n_sec - 1

    q_s[me_d] = matmul(hidden, p_out[3]).astype(jnp.bfloat16)
    for c in q_x:
        c.start()
    back = dgdu[0]
    for slot in range(4):
        e_s[owners[slot]] = matmul_nt(back, p_in[slot]).astype(jnp.bfloat16)
    for c in e_x:
        c.start()

    for c in range(CHUNKS):
        q_x[c].wait_recv()

        @pl.loop(0, part // 16)
        def _(t, c=c):
            at = pl.ds(pl.multiple_of(own + c * part + t * 16, 16), 16)
            near = pl.ds(pl.multiple_of(c * part + t * 16, 16), 16)
            for j in range(n_dp):
                total = q_s[j, at, :].astype(jnp.float32) + q_r[j, near, :].astype(jnp.float32)
                y_s[near, j * cols : (j + 1) * cols] = (
                    xf[j, at, :].astype(jnp.float32) + total
                ).astype(jnp.bfloat16)

        @pl.when(jnp.logical_not(last))
        def _(c=c):
            y_m[c][0].start()

    for c in range(CHUNKS):
        e_x[c].wait_recv()

        @pl.loop(0, part // 16)
        def _(t, c=c):
            at = pl.ds(pl.multiple_of(own + c * part + t * 16, 16), 16)
            near = pl.ds(pl.multiple_of(c * part + t * 16, 16), 16)
            xs = [xb[j, at, :].astype(jnp.float32) for j in range(n_dp)]
            total = functools.reduce(jnp.add, [p * p for p in xs])
            inv = 1.0 / (n_dp * cols)
            factor = lax.rsqrt(jnp.sum(total, axis=-1, keepdims=True) * inv + NORM_EPS)
            scaled = [
                gain[:, j * cols : (j + 1) * cols]
                * (e_s[j, at, :].astype(jnp.float32) + e_r[j, near, :].astype(jnp.float32))
                for j in range(n_dp)
            ]
            inner = functools.reduce(jnp.add, [s * x for s, x in zip(scaled, xs)])
            mean = jnp.sum(inner, axis=-1, keepdims=True) * inv
            tail = factor * factor * factor * mean
            for j in range(n_dp):
                dx_s[near, j * cols : (j + 1) * cols] = (
                    dy[j, at, :].astype(jnp.float32) + factor * scaled[j] - xs[j] * tail
                ).astype(jnp.bfloat16)

        @pl.when(jnp.logical_not(first))
        def _(c=c):
            dx_m[c][0].start()

    for c, on in share:
        c.wait_recv()
        on.start()
    h_x[0].wait_recv()
    h_on_y.start()
    h_y[1].wait_recv()
    h_on_x.start()
    g_x[0].wait_recv()
    g_on_y.start()
    g_y[1].wait_recv()
    g_on_x.start()

    @pl.when(first)
    def _():
        y_b[...] = jnp.zeros_like(y_b)

    @pl.when(jnp.logical_not(first))
    def _():
        for c, on in y_m:
            c.wait_recv()
            on.start()

    @pl.when(last)
    def _():
        dx_b[...] = jnp.zeros_like(dx_b)

    @pl.when(jnp.logical_not(last))
    def _():
        for c, on in dx_m:
            c.wait_recv()
            on.start()

    for _, on in share:
        on.wait_recv()
    h_x[1].wait_recv()
    h_y[0].wait_recv()
    h_on_y.wait_recv()
    h_on_x.wait_recv()
    tokens = n_dp * rows
    g_out[...] = matmul_tn(h_all[...].reshape(tokens, ff), dy_all[...].reshape(tokens, cols))

    @pl.loop(0, ff // 32)
    def _(t):
        at = pl.ds(pl.multiple_of(t * 32, 32), 32)
        keep_m, keep_v = decayed(c_out[at, :], sm, sv)
        g_out[at, :] = updated(g_out[at, :], keep_m, keep_v, tokens)

    g_x[1].wait_recv()
    g_y[0].wait_recv()
    near = 3 * rows
    g_in[...] = matmul_tn(n_all[:3].reshape(near, cols), dgdu[:3].reshape(near, 2 * ff))
    g_on_y.wait_recv()
    g_on_x.wait_recv()
    g_in[...] += matmul_tn(n_all[3], dgdu[3])

    @pl.when(jnp.logical_not(first))
    def _():
        for c, on in y_m:
            on.wait_recv()
            on.wait_send()
        for c, _ in dx_m:
            c.wait_send()

    @pl.when(jnp.logical_not(last))
    def _():
        for c, on in dx_m:
            on.wait_recv()
            on.wait_send()
        for c, _ in y_m:
            c.wait_send()

    for group in ((a_x, a_y, a_on_y, a_on_x), (d_x, d_y, d_on_y, d_on_x),
                  (h_x, h_y, h_on_y, h_on_x), (g_x, g_y, g_on_y, g_on_x)):
        for c in (*group[0], *group[1], group[2], group[3]):
            c.wait_send()
    for c, on in share:
        c.wait_send()
        on.wait_send()
    for c in (*q_x, *e_x):
        c.wait_send()


def finish_kernel(
    tokens, y_b, dx_b, u_out, g_in, m_in, v_in,
    y_hbm, dx_hbm, u_in_hbm, u_out_hbm, u_in, sem,
):
    _, cols, ff = u_in.shape
    copies = [
        pltpu.make_async_copy(src, dst, sem.at[i])
        for i, (src, dst) in enumerate(((y_b, y_hbm), (dx_b, dx_hbm), (u_out, u_out_hbm)))
    ]
    for c in copies:
        c.start()
    pieces = 2
    tall = cols // pieces
    for piece in range(pieces):
        @pl.loop(0, tall // 32)
        def _(t, piece=piece):
            at = pl.ds(pl.multiple_of(piece * tall + t * 32, 32), 32)
            for k in range(2):
                lanes = slice(k * ff, (k + 1) * ff)
                u_in[k, at, :] = updated(g_in[at, lanes], m_in[at, lanes], v_in[at, lanes], tokens)

        at = pl.ds(piece * tall, tall)
        c = pltpu.make_async_copy(u_in.at[:, at], u_in_hbm.at[:, at], sem.at[3 + piece])
        c.start()
        copies.append(c)
    for c in copies:
        c.wait()


def tick(
    n_sec, n_dp,
    forward_input, backward_input, output_grad, norm_gain,
    in_weight, out_weight, in_codes, out_codes, in_scales, out_scales, section_lags,
):
    xf, xb, dy = forward_input[0], backward_input[0], output_grad[0]
    rows, width = xf.shape
    _, cols, ff = in_weight.shape[1:]
    half_r = rows // 2
    bf, f32 = jnp.bfloat16, jnp.float32
    vmem = pl.BlockSpec(memory_space=pltpu.VMEM)
    hbm = pl.BlockSpec(memory_space=pltpu.HBM)
    V = pltpu.VMEM
    wide = (n_dp, rows, cols)
    n_remote = 4 * 6 + 12 + 2 * CHUNKS + 4 * CHUNKS
    held = pl.pallas_call(
        functools.partial(tick_kernel, n_sec),
        out_shape=(
            V((rows, width), bf),
            V((rows, width), bf),
            V((ff, cols), f32),
            V((cols, 2 * ff), f32),
            V((cols, 2 * ff), f32),
            V((cols, 2 * ff), f32),
        ),
        in_specs=[pl.BlockSpec(memory_space=pltpu.SMEM), vmem, vmem, vmem] + [hbm] * 7,
        out_specs=(vmem,) * 6,
        scratch_shapes=[
            V(wide, bf), V(wide, bf), V(wide, bf),
            V((2, cols, ff), f32), V((ff, cols), f32),
            V((2, cols, ff), jnp.int32), V((ff, cols), jnp.int32),
            V((4, cols, 128), f32),
            V((n_dp, cols, 2 * ff), bf), V((n_dp, ff, cols), bf),
            V((n_dp, 2 * rows, cols), bf),
            V((2 * rows, 2 * ff), f32), V((rows, ff), f32), V((rows, ff), bf),
            V((n_dp, rows, 2 * ff), bf), V((n_dp, rows, ff), bf), V(wide, bf), V(wide, bf),
            V(wide, bf), V((n_dp, half_r, cols), bf), V(wide, bf), V((n_dp, half_r, cols), bf),
            V((half_r, width), bf), V((half_r, width), bf),
            pltpu.SemaphoreType.DMA((6 + 3 * n_dp,)),
            pltpu.SemaphoreType.DMA((n_remote,)),
            pltpu.SemaphoreType.DMA((n_remote,)),
        ],
        compiler_params=pltpu.CompilerParams(
            collective_id=0, has_side_effects=True, vmem_limit_bytes=61200000
        ),
    )(
        section_lags, norm_gain, jnp.swapaxes(in_scales[0], 2, 3).reshape(4, 1, cols), out_scales[0],
        xf, xb, dy, in_weight[0], out_weight[0], in_codes[0], out_codes[0],
    )
    outs = pl.pallas_call(
        functools.partial(finish_kernel, rows * n_dp),
        out_shape=(
            jax.ShapeDtypeStruct((rows, width), bf),
            jax.ShapeDtypeStruct((rows, width), bf),
            jax.ShapeDtypeStruct((2, cols, ff), f32),
            jax.ShapeDtypeStruct((ff, cols), f32),
        ),
        in_specs=[vmem] * 6,
        out_specs=(hbm,) * 4,
        scratch_shapes=[V((2, cols, ff), f32), pltpu.SemaphoreType.DMA((5,))],
        compiler_params=pltpu.CompilerParams(vmem_limit_bytes=16 * 1024 * 1024),
    )(*held)
    return tuple(o[None] for o in outs)


def solution(mesh):
    in_specs = (
        P("section", "dp", None),
        P("section", "dp", None),
        P("section", "dp", None),
        P("section", None),
        P("section", None, "dp", "hid"),
        P("section", "hid", "dp"),
        P("section", None, "dp", "hid"),
        P("section", "hid", "dp"),
        P("section", None, None, "dp", "hid"),
        P("section", None, "hid", "dp"),
        P("section"),
    )
    out_specs = (
        P("section", "dp", None),
        P("section", "dp", None),
        P("section", None, "dp", "hid"),
        P("section", "hid", "dp"),
    )
    if (mesh.shape["dp"], mesh.shape["hid"]) == (4, 2):
        body = functools.partial(tick, mesh.shape["section"], mesh.shape["dp"])
    else:
        body = local
    return jax.shard_map(body, mesh=mesh, in_specs=in_specs, out_specs=out_specs, check_vma=False)
```
